32 devices in a mesh: dp: 2 (over x), expert: 16 (over z, y, core).
Axes of the slice: x: 2, y: 2, z: 4, core: 2. Of those that a mesh axis runs over, the one named last changes fastest.
Arguments:
- tokens: bfloat16 [8192, 1024], P(('dp', 'expert')), may hold values from -6 to 6
- modulation: bfloat16 [32, 2, 1024], P(('dp', 'expert')), may hold values from -3 to 3
- router_weight: bfloat16 [1024, 16], replicated, may hold values from -0.1875 to 0.1875
- weight_in: bfloat16 [16, 1024, 4096], P('expert', None, 'dp'), may hold values from -0.1875 to 0.1875
- weight_out: bfloat16 [16, 4096, 1024], P('expert', 'dp'), may hold values from -0.09375 to 0.09375
- chosen: int32 [2, 16, 256], P('dp'), may hold values from 0 to 4095, as said below
- grad_out: bfloat16 [8192, 1024], P(('dp', 'expert')), may hold values from -4 to 4
Outputs:
- grad_tokens: bfloat16 [8192, 1024], P(('dp', 'expert'))
- grad_mod: float32 [32, 2, 1024], P(('dp', 'expert'))
- grad_router: float32 [1024, 16], replicated
- grad_weight_in: bfloat16 [16, 1024, 4096], P('expert', None, 'dp')
- grad_weight_out: bfloat16 [16, 4096, 1024], P('expert', 'dp')
The draws below stay inside these ranges and needn't reach their ends.
Inputs may be any that keep to these rules, and one draw needn't show every extreme that they name: `chosen`: for each slice and expert the 256 positions are distinct; at most 32 of them lie in one image's 256 tokens, and in one image exactly 32.
All inputs are finite; a program needn't handle non-finite values.
Results may differ from the reference program's by a relative error of at most 0.008.
Values may be sent and summed in bfloat16 or wider, within the bound.
No kernel may reach another device: no remote copies, remote signals or barrier semaphores. Data moves between devices by JAX's collectives and lax.ppermute only.
A program may use at most 128 MiB of HBM per device.

```python
import jax
import jax.numpy as jnp
from jax import lax

D = 1024
HID = 4096
TOK_DEV = 256
EXPERTS = 16
IMAGES = 32
TOKENS = 8192
SLICE = 4096
CAP = 256
MOST = 32
N_DP = 2


def draw_chosen(key, part):
    slices = IMAGES // EXPERTS
    images = SLICE // TOK_DEV
    pairs = images // 2

    def one_list(list_key):
        order_key, split_key, rows_key = jax.random.split(list_key, 3)
        order = jax.random.permutation(order_key, images)
        splits = jax.random.randint(split_key, (pairs,), 0, MOST + 1)
        splits = splits.at[0].set(MOST)
        pair_counts = jnp.stack([splits, MOST - splits], axis=1).reshape(-1)
        counts = jnp.zeros((images,), jnp.int32).at[order].set(pair_counts.astype(jnp.int32))
        row_keys = jax.random.split(rows_key, images)
        picked = jax.vmap(lambda each_key: jax.random.permutation(each_key, TOK_DEV)[:MOST])(row_keys)
        slot_index = jnp.arange(MOST, dtype=jnp.int32)[None, :]
        is_valid = slot_index < counts[:, None]
        global_rows = jnp.arange(images, dtype=jnp.int32)[:, None] * TOK_DEV + picked.astype(jnp.int32)
        ranking = jnp.where(is_valid, 0, 1) * (images * MOST) + jnp.arange(images * MOST, dtype=jnp.int32).reshape(images, MOST)
        keep = jnp.argsort(ranking.reshape(-1), stable=True)[:CAP]
        return global_rows.reshape(-1)[keep].astype(jnp.int32)
    list_keys = jax.random.split(jax.random.fold_in(key, 17), slices * EXPERTS)
    return jax.vmap(one_list)(list_keys).reshape(slices, EXPERTS, CAP).astype(jnp.int32)


def block_levels(key, extent, shards, low, largest):
    gain = 1.0
    for dim, shards_of in shards:
        draws = jax.random.uniform(jax.random.fold_in(jax.random.fold_in(key, 6), dim), (shards_of,), jnp.float32, low / len(shards), largest / len(shards))
        gain = gain * jnp.repeat(jnp.exp(draws), extent[dim] // shards_of).reshape((-1,) + (1,) * (len(extent) - 1 - dim))
    return gain


def noise(rng, shape, scale, most, cuts=(), kind=jnp.bfloat16):
    level = block_levels(rng, shape, cuts, -0.22, 0.18) if cuts else 1.0
    array = jax.random.normal(rng, shape, jnp.float32) * scale * level
    return jnp.minimum(jnp.maximum(array, -most), most).astype(kind)


def setup_inputs(seed: int = 0) -> dict:
    arg_keys = jax.random.split(jax.random.key(seed), 8)
    return {
        "tokens": noise(arg_keys[0], (TOKENS, D), 1.0, 6.0, ((0, 32),)),
        "modulation": noise(arg_keys[1], (IMAGES, 2, D), 0.5, 3.0, ((0, 32),)),
        "router_weight": noise(arg_keys[2], (D, EXPERTS), D ** -0.5, 0.1875),
        "weight_in": noise(arg_keys[3], (EXPERTS, D, HID), D ** -0.5, 0.1875, ((0, 16), (2, 2))),
        "weight_out": noise(arg_keys[4], (EXPERTS, HID, D), HID ** -0.5, 0.09375, ((0, 16), (1, 2))),
        "chosen": draw_chosen(jax.random.fold_in(arg_keys[7], 71), 0),
        "grad_out": noise(arg_keys[6], (TOKENS, D), 0.5, 4.0, ((0, 32),)),
    }


gelu_root = 0.7978845608028654
gelu_cube = 0.044715
norm_eps = 1e-06

def gelu_value(values):
    inner = gelu_root * (values + gelu_cube * values * values * values)
    return 0.5 * values * (1.0 + jnp.tanh(inner))

def gelu_slope(values):
    tangent = jnp.tanh(gelu_root * (values + gelu_cube * values * values * values))
    return 0.5 * (1.0 + tangent) + 0.5 * values * (1.0 - tangent * tangent) * gelu_root * (1.0 + 3.0 * gelu_cube * values * values)

def expert_terms(rows_u, rows_g, rows_p, first_w, second_w):
    preact = jnp.dot(rows_u, first_w, preferred_element_type=jnp.float32)
    hidden = gelu_value(preact).astype(jnp.bfloat16)
    upstream = lax.dot_general(rows_g, second_w, (((1,), (1,)), ((), ())), preferred_element_type=jnp.float32)
    score_sum = lax.optimization_barrier(jnp.sum(hidden.astype(jnp.float32) * upstream, axis=1))
    prob_col = rows_p.astype(jnp.float32)[:, None]
    grad_y = (prob_col * rows_g.astype(jnp.float32)).astype(jnp.bfloat16)
    grad_pre = (prob_col * upstream * gelu_slope(preact)).astype(jnp.bfloat16)
    return (hidden, score_sum, grad_y, grad_pre)

def reference(tokens, modulation, router_weight, weight_in, weight_out, chosen, grad_out):
    x_float = tokens.astype(jnp.float32)
    average = lax.optimization_barrier(jnp.mean(x_float, axis=1, keepdims=True))
    centred = x_float - average
    spread = lax.optimization_barrier(jnp.mean(centred * centred, axis=1, keepdims=True))
    inverse = lax.rsqrt(spread + norm_eps)
    normed = centred * inverse
    mod_float = modulation.astype(jnp.float32)
    shift_rows = jnp.repeat(mod_float[:, 0], TOK_DEV, axis=0)
    scale_rows = jnp.repeat(mod_float[:, 1], TOK_DEV, axis=0)
    normal_u = (normed * (1.0 + scale_rows) + shift_rows).astype(jnp.bfloat16)
    gate_prob = jax.nn.sigmoid(jnp.dot(normal_u, router_weight, preferred_element_type=jnp.float32)).astype(jnp.bfloat16)
    slice_start = jnp.arange(N_DP, dtype=jnp.int32) * SLICE
    global_ids = chosen + slice_start[:, None, None]
    per_expert = jnp.transpose(global_ids, (1, 0, 2)).reshape(EXPERTS, N_DP * CAP).astype(jnp.int32)
    expert_index = jnp.arange(EXPERTS, dtype=jnp.int32)

    def one_expert(packed):
        first_w, second_w, row_ids, index = packed
        rows_u = normal_u[row_ids]
        rows_g = grad_out[row_ids]
        rows_p = gate_prob[row_ids, index]
        hidden, score_sum, grad_y, grad_pre = expert_terms(rows_u, rows_g, rows_p, first_w, second_w)
        grad_first = lax.dot_general(rows_u, grad_pre, (((0,), (0,)), ((), ())), preferred_element_type=jnp.float32).astype(jnp.bfloat16)
        grad_second = lax.dot_general(hidden, grad_y, (((0,), (0,)), ((), ())), preferred_element_type=jnp.float32).astype(jnp.bfloat16)
        grad_rows = lax.dot_general(grad_pre, first_w, (((1,), (1,)), ((), ())), preferred_element_type=jnp.float32).astype(jnp.bfloat16)
        return (grad_first, grad_second, grad_rows, score_sum.astype(jnp.bfloat16))
    grads_first, grads_second, grad_rows, scores = lax.map(one_expert, (weight_in, weight_out, per_expert, expert_index))
    flat_ids = per_expert.reshape(-1)
    flat_experts = jnp.repeat(expert_index, N_DP * CAP)
    grad_u = jnp.zeros((TOKENS, D), jnp.float32).at[flat_ids].add(grad_rows.reshape(-1, D).astype(jnp.float32))
    prob_sel = gate_prob[flat_ids, flat_experts].astype(jnp.float32)
    logit_terms = scores.reshape(-1).astype(jnp.float32) * prob_sel * (1.0 - prob_sel)
    grad_logit = jnp.zeros((TOKENS, EXPERTS), jnp.float32).at[flat_ids, flat_experts].add(logit_terms)
    grad_u = grad_u + jnp.dot(grad_logit, router_weight.astype(jnp.float32).T, precision=lax.Precision.HIGHEST)
    grad_router = jnp.dot(normal_u.astype(jnp.float32).T, grad_logit, precision=lax.Precision.HIGHEST)
    grad_image = grad_u.reshape(IMAGES, TOK_DEV, D)
    grad_shift = lax.optimization_barrier(jnp.sum(grad_image, axis=1))
    grad_scale = lax.optimization_barrier(jnp.sum(grad_image * normed.reshape(IMAGES, TOK_DEV, D), axis=1))
    grad_mod = jnp.stack([grad_shift, grad_scale], axis=1)
    grad_norm = grad_u * (1.0 + scale_rows)
    centre_term = lax.optimization_barrier(jnp.mean(grad_norm, axis=1, keepdims=True))
    slope_term = lax.optimization_barrier(jnp.mean(grad_norm * normed, axis=1, keepdims=True))
    grad_tokens = (grad_out.astype(jnp.float32) + (grad_norm - centre_term - normed * slope_term) * inverse).astype(jnp.bfloat16)
    return (grad_tokens, grad_mod, grad_router, grads_first, grads_second)
```

```python
import jax
import jax.numpy as jnp
from jax import lax
from jax.sharding import PartitionSpec as P

gelu_root = 0.7978845608028654
gelu_cube = 0.044715
norm_eps = 1e-06


def gelu_both(values):
    tangent = jnp.tanh(gelu_root * (values + gelu_cube * values * values * values))
    value = 0.5 * values * (1.0 + tangent)
    slope = 0.5 * (1.0 + tangent) + 0.5 * values * (1.0 - tangent * tangent) * gelu_root * (
        1.0 + 3.0 * gelu_cube * values * values
    )
    return value, slope


def swap_dp(values):
    count = lax.axis_size("dp")
    return lax.ppermute(values, "dp", [(i, count - 1 - i) for i in range(count)])


def contract(left, right, dims):
    return lax.dot_general(left, right, (dims, ((), ())), preferred_element_type=jnp.float32)


def body(tokens, modulation, router_weight, weight_in, weight_out, chosen, grad_out):
    tok_count, width = tokens.shape
    experts = lax.axis_size("expert")
    halves = lax.axis_size("dp")
    me = lax.axis_index("expert")
    most = 2 * tok_count // experts
    cap = chosen.shape[2]
    bf16, f32 = jnp.bfloat16, jnp.float32

    local_row = chosen[0] - me * tok_count
    token_id = jnp.arange(tok_count, dtype=jnp.int32)
    member = jnp.any(local_row[:, :, None] == token_id, axis=1)
    before = (token_id[:, None] < token_id[None, :]).astype(bf16)
    rank = contract(member.astype(bf16), before, ((1,), (0,))).astype(jnp.int32)
    slot = jnp.where(member, rank, -1)
    slot_id = jnp.arange(most, dtype=jnp.int32)
    select = (slot[:, None, :] == slot_id[None, :, None]).astype(bf16)
    select = select.reshape(experts * most, tok_count)

    mine = lax.dynamic_index_in_dim(chosen[0], me, 0, keepdims=False)
    image_id = jnp.arange(experts, dtype=jnp.int32)
    counts = jnp.sum((mine[None, :] // tok_count == image_id[:, None]).astype(jnp.int32), axis=1)
    starts = jnp.sum(jnp.where(image_id[:, None] > image_id[None, :], counts[None, :], 0), axis=1)
    place = jnp.where(slot_id[None, :] < counts[:, None], starts[:, None] + slot_id[None, :], -1)
    compact = (place.reshape(1, -1) == jnp.arange(cap, dtype=jnp.int32)[:, None]).astype(bf16)

    x_float = tokens.astype(f32)
    average = jnp.mean(x_float, axis=1, keepdims=True)
    centred = x_float - average
    spread = jnp.mean(centred * centred, axis=1, keepdims=True)
    inverse = lax.rsqrt(spread + norm_eps)
    normed = centred * inverse
    shift_mod = modulation[0, 0].astype(f32)
    scale_mod = modulation[0, 1].astype(f32)
    normal_u = (normed * (1.0 + scale_mod) + shift_mod).astype(bf16)

    def exchange(rows):
        rows = rows.reshape(experts, most, width)
        rows = lax.all_to_all(rows, "expert", split_axis=0, concat_axis=0, tiled=True)
        return rows.reshape(experts * most, width)

    def gather_rows(source):
        sent = contract(select, source, ((1,), (0,))).astype(bf16)
        got = contract(compact, exchange(sent), ((1,), (0,))).astype(bf16)
        return jnp.concatenate([got, swap_dp(got)], axis=0)

    rows_u = gather_rows(normal_u)
    rows_g = gather_rows(grad_out)
    first_w, second_w = weight_in[0], weight_out[0]
    router_col = lax.dynamic_index_in_dim(router_weight, me, 1, keepdims=False).astype(f32)
    logits = jnp.sum(rows_u.astype(f32) * router_col, axis=1)
    gate = jax.nn.sigmoid(logits).astype(bf16).astype(f32)[:, None]

    preact = contract(rows_u, first_w, ((1,), (0,)))
    upstream = contract(rows_g, second_w, ((1,), (1,)))
    value, slope = gelu_both(preact)
    hidden = value.astype(bf16)
    score_part = jnp.sum(hidden.astype(f32) * upstream, axis=1, keepdims=True)
    grad_y = (gate * rows_g.astype(f32)).astype(bf16)
    grad_pre = (gate * upstream * slope).astype(bf16)
    logit_part = score_part * gate * (1.0 - gate)
    rows_part = contract(grad_pre, first_w, ((1,), (1,))) + logit_part * router_col

    total = rows_part[:cap] + swap_dp(rows_part[cap:].astype(bf16)).astype(f32)
    back = contract(compact, total.astype(bf16), ((0,), (0,))).astype(bf16)
    grad_ret = exchange(back)

    column = jnp.sum(rows_u.astype(f32) * logit_part, axis=0)
    columns = lax.all_to_all(
        jnp.broadcast_to(column, (halves * experts, width)), ("dp", "expert"), 0, 0, tiled=True
    )
    grad_router = jnp.sum(columns.reshape(halves, experts, width), axis=0).T

    grad_weight_in = contract(rows_u, grad_pre, ((0,), (0,))).astype(bf16)[None]
    grad_weight_out = contract(hidden, grad_y, ((0,), (0,))).astype(bf16)[None]

    grad_u = contract(select, grad_ret, ((0,), (0,)))
    grad_shift = jnp.sum(grad_u, axis=0)
    grad_scale = jnp.sum(grad_u * normed, axis=0)
    grad_mod = jnp.stack([grad_shift, grad_scale], axis=0)[None]
    grad_norm = grad_u * (1.0 + scale_mod)
    centre_term = jnp.mean(grad_norm, axis=1, keepdims=True)
    slope_term = jnp.mean(grad_norm * normed, axis=1, keepdims=True)
    grad_tokens = (
        grad_out.astype(f32) + (grad_norm - centre_term - normed * slope_term) * inverse
    ).astype(bf16)
    return (grad_tokens, grad_mod, grad_router, grad_weight_in, grad_weight_out)


def solution(mesh):
    placed = (
        P(("dp", "expert"), None),
        P(("dp", "expert"), None, None),
        P(),
        P("expert", None, "dp"),
        P("expert", "dp", None),
        P("dp", None, None),
        P(("dp", "expert"), None),
    )
    return jax.shard_map(
        body,
        mesh=mesh,
        in_specs=placed,
        out_specs=(
            P(("dp", "expert"), None),
            P(("dp", "expert"), None, None),
            P(),
            P("expert", None, "dp"),
            P("expert", "dp", None),
        ),
        check_vma=False,
    )
```

```python
import jax
import jax.numpy as jnp
from jax import lax
from jax.experimental import pallas as pl
from jax.experimental.pallas import tpu as pltpu
from jax.sharding import PartitionSpec as P

gelu_root = 0.7978845608028654
gelu_cube = 0.044715
norm_eps = 1e-06
bf16, f32, i32 = jnp.bfloat16, jnp.float32, jnp.int32

back_parts = 2
hidden_tile = 512


def gelu_both(values):
    tangent = jnp.tanh(gelu_root * (values + gelu_cube * values * values * values))
    value = 0.5 * values * (1.0 + tangent)
    slope = 0.5 * (1.0 + tangent) + 0.5 * values * (1.0 - tangent * tangent) * gelu_root * (
        1.0 + 3.0 * gelu_cube * values * values
    )
    return value, slope


def contract(left, right, left_dim, right_dim):
    return lax.dot_general(
        left, right, (((left_dim,), (right_dim,)), ((), ())), preferred_element_type=f32
    )


def iota(shape, dim):
    return lax.broadcasted_iota(i32, shape, dim)


def normalise(tokens):
    x_float = tokens.astype(f32)
    centred = x_float - jnp.mean(x_float, axis=1, keepdims=True)
    spread = jnp.mean(centred * centred, axis=1, keepdims=True)
    inverse = lax.rsqrt(spread + norm_eps)
    return centred * inverse, inverse


def prep_kernel(me_ref, chosen_ref, tokens_ref, mod_ref, grad_ref, *outs):
    experts, cap = chosen_ref.shape
    tok_count = tokens_ref.shape[0]
    most = 2 * tok_count // experts
    shift = tok_count.bit_length() - 1
    u_outs, g_outs = outs[:experts], outs[experts : 2 * experts]
    select_ref, compact_ref, slot_ref = outs[2 * experts :]
    me = me_ref[0]

    lanes = max(128, experts)
    padded = chosen_ref[...]
    if lanes > experts:
        padded = jnp.concatenate([padded, jnp.zeros((lanes - experts, cap), i32)], axis=0)
    listed = jnp.transpose(padded)
    local = listed - me * tok_count
    token_row = iota((cap, tok_count), 1)
    member = [
        jnp.sum((local[:, e : e + 1] == token_row).astype(f32), axis=0, keepdims=True)
        for e in range(experts)
    ]
    member = jnp.concatenate(member, axis=0)
    before = (iota((tok_count, tok_count), 0) < iota((tok_count, tok_count), 1)).astype(bf16)
    rank = contract(member.astype(bf16), before, 1, 0)
    slot_ref[...] = jnp.where(member > 0.5, rank.astype(i32), -1)
    for k in range(experts):
        row = slot_ref[pl.ds(me ^ k, 1), :]
        select_ref[k * most : (k + 1) * most, :] = (
            (row == iota((most, tok_count), 0)).astype(f32).astype(bf16)
        )

    mine = jnp.sum(jnp.where(iota((cap, lanes), 1) == me, listed, 0), axis=1, keepdims=True)
    source = lax.shift_right_logical(mine, shift) ^ me
    lane = iota((1, experts * most), 1)
    block = lax.shift_right_logical(lane, most.bit_length() - 1)
    offset = lane & (most - 1)
    count = jnp.sum((source == block).astype(f32), axis=0, keepdims=True).astype(i32)
    start = jnp.sum((source < block).astype(f32), axis=0, keepdims=True).astype(i32)
    place = jnp.where(offset < count, start + offset, -1)
    compact_ref[...] = (
        (iota((cap, experts * most), 0) == place).astype(f32).astype(bf16)
    )

    normed, _ = normalise(tokens_ref[...])
    mod = mod_ref[...].astype(f32)
    normal_u = (normed * (1.0 + mod[1:2]) + mod[0:1]).astype(bf16)
    select = select_ref[...]
    sent = contract(select, normal_u, 1, 0).astype(bf16)
    for k in range(experts):
        u_outs[k][...] = sent[k * most : (k + 1) * most]
    sent = contract(select, grad_ref[...], 1, 0).astype(bf16)
    for k in range(experts):
        g_outs[k][...] = sent[k * most : (k + 1) * most]


def compact_kernel(compact_ref, *refs):
    rows = jnp.concatenate([ref[...] for ref in refs[:-1]], axis=0)
    refs[-1][...] = contract(compact_ref[...], rows, 1, 0).astype(bf16)


def rows_kernel(
    me_ref, u_ref, g_ref, router_ref, first_ref, second_ref, hidden_ref, pre_ref, y_ref, column_ref,
    *rest,
):
    parts, (gate_ref, score_ref, acc_ref) = rest[:-3], rest[-3:]
    step = pl.program_id(0)
    me = me_ref[0]

    @pl.when(step == 0)
    def _():
        probs = jax.nn.sigmoid(contract(u_ref[...], router_ref[...], 1, 0)).astype(bf16).astype(f32)
        gate = jnp.sum(jnp.where(iota(probs.shape, 1) == me, probs, 0.0), axis=1, keepdims=True)
        gate_ref[...] = gate
        score_ref[...] = jnp.zeros_like(score_ref)
        y_ref[...] = (gate * g_ref[...].astype(f32)).astype(bf16)

    preact = contract(u_ref[...], first_ref[0], 1, 0)
    upstream = contract(g_ref[...], second_ref[0], 1, 1)
    value, slope = gelu_both(preact)
    hidden = value.astype(bf16)
    hidden_ref[...] = hidden
    score_ref[...] += jnp.sum(hidden.astype(f32) * upstream, axis=1, keepdims=True)
    grad_pre = (gate_ref[...] * upstream * slope).astype(bf16)
    pre_ref[...] = grad_pre
    back = contract(grad_pre, first_ref[0], 1, 1)

    @pl.when(step == 0)
    def _():
        acc_ref[...] = back

    @pl.when(step > 0)
    def _():
        acc_ref[...] += back

    @pl.when(step == pl.num_programs(0) - 1)
    def _():
        gate = gate_ref[...]
        logit = score_ref[...] * gate * (1.0 - gate)
        experts = router_ref.shape[1]
        pick = (iota((8, experts), 1) == me).astype(f32).astype(bf16)
        router_row = contract(pick, router_ref[...], 1, 1)[0:1]
        total = acc_ref[...] + logit * router_row
        size = total.shape[1] // len(parts)
        for i, part in enumerate(parts):
            part[...] = total[:, i * size : (i + 1) * size].astype(part.dtype)
        column_ref[...] = jnp.sum(u_ref[...].astype(f32) * logit, axis=0, keepdims=True)


def weights_kernel(
    u_own, u_other, pre_own, pre_other, hidden_own, hidden_other, y_own, y_other,
    first_ref, second_ref, turned_ref,
):
    @pl.when(pl.program_id(0) == 0)
    def _():
        turned_ref[...] = jnp.transpose(jnp.concatenate([u_own[...], u_other[...]], axis=0))

    pre = jnp.concatenate([pre_own[...], pre_other[...]], axis=0)
    first_ref[0] = contract(turned_ref[...], pre, 1, 0).astype(bf16)
    hidden = jnp.transpose(jnp.concatenate([hidden_own[...], hidden_other[...]], axis=0))
    grad_y = jnp.concatenate([y_own[...], y_other[...]], axis=0)
    second_ref[0] = contract(hidden, grad_y, 1, 0).astype(bf16)


def spread_kernel(compact_ref, own_ref, other_ref, *outs):
    total = (own_ref[...] + other_ref[...].astype(f32)).astype(bf16)
    rows = contract(compact_ref[...], total, 0, 0).astype(bf16)
    most = rows.shape[0] // len(outs)
    for k, out in enumerate(outs):
        out[...] = rows[k * most : (k + 1) * most]


def final_kernel(select_ref, tokens_ref, mod_ref, grad_ref, *refs):
    blocks, (token_out, mod_out) = refs[:-2], refs[-2:]
    experts = len(blocks) // back_parts
    parts = [
        jnp.concatenate([ref[...] for ref in blocks[i * experts : (i + 1) * experts]], axis=0)
        for i in range(back_parts)
    ]
    rows = jnp.concatenate(parts, axis=1)
    grad_u = contract(select_ref[...], rows, 0, 0)
    normed, inverse = normalise(tokens_ref[...])
    mod = mod_ref[...].astype(f32)
    mod_out[0, 0:1, :] = jnp.sum(grad_u, axis=0, keepdims=True)
    mod_out[0, 1:2, :] = jnp.sum(grad_u * normed, axis=0, keepdims=True)
    grad_norm = grad_u * (1.0 + mod[1:2])
    centre = jnp.mean(grad_norm, axis=1, keepdims=True)
    along = jnp.mean(grad_norm * normed, axis=1, keepdims=True)
    token_out[...] = (
        grad_ref[...].astype(f32) + (grad_norm - centre - normed * along) * inverse
    ).astype(bf16)


scalar_spec = pl.BlockSpec(memory_space=pltpu.SMEM)
big = pltpu.CompilerParams(vmem_limit_bytes=56 * 1024 * 1024)


def swap_dp(values):
    count = lax.axis_size("dp")
    return lax.ppermute(values, "dp", [(i, count - 1 - i) for i in range(count)])


def exchange(blocks):
    count = len(blocks)
    order = sorted(range(1, count), reverse=True)
    got = {0: blocks[0]}
    for k in order:
        got[k] = lax.ppermute(blocks[k], "expert", [(i, i ^ k) for i in range(count)])
    return [got[k] for k in range(count)]


def body(tokens, modulation, router_weight, weight_in, weight_out, chosen, grad_out):
    tok_count, width = tokens.shape
    experts = lax.axis_size("expert")
    halves = lax.axis_size("dp")
    most = 2 * tok_count // experts
    cap = chosen.shape[2]
    units = weight_in.shape[2]
    me = lax.axis_index("expert").reshape(1).astype(i32)
    shape = jax.ShapeDtypeStruct

    sent = pl.pallas_call(
        prep_kernel,
        in_specs=[scalar_spec] + [pl.BlockSpec()] * 4,
        out_shape=[shape((most, width), bf16)] * (2 * experts)
        + [shape((experts * most, tok_count), bf16), shape((cap, experts * most), bf16)],
        scratch_shapes=[pltpu.VMEM((experts, tok_count), i32)],
        compiler_params=big,
        name="prep",
    )(me, chosen[0], tokens, modulation[0], grad_out)
    select, compact = sent[2 * experts :]

    gather_rows = pl.pallas_call(
        compact_kernel, out_shape=shape((cap, width), bf16), compiler_params=big, name="compact"
    )
    got_u = exchange(sent[:experts])
    got_g = exchange(sent[experts : 2 * experts])
    u_own = gather_rows(compact, *got_u)
    u_other = swap_dp(u_own)
    g_own = gather_rows(compact, *got_g)
    g_other = swap_dp(g_own)

    tile = min(hidden_tile, units)
    part = width // back_parts

    def rows_call(kind):
        def whole(*size):
            return pl.BlockSpec(size, lambda i: (0,) * len(size))

        return pl.pallas_call(
            rows_kernel,
            grid=(units // tile,),
            in_specs=[
                scalar_spec,
                whole(cap, width),
                whole(cap, width),
                whole(width, experts),
                pl.BlockSpec((1, width, tile), lambda i: (0, 0, i)),
                pl.BlockSpec((1, tile, width), lambda i: (0, i, 0)),
            ],
            out_specs=[
                pl.BlockSpec((cap, tile), lambda i: (0, i)),
                pl.BlockSpec((cap, tile), lambda i: (0, i)),
                whole(cap, width),
                whole(1, width),
            ]
            + [whole(cap, part)] * back_parts,
            out_shape=[
                shape((cap, units), bf16),
                shape((cap, units), bf16),
                shape((cap, width), bf16),
                shape((1, width), f32),
            ]
            + [shape((cap, part), kind)] * back_parts,
            scratch_shapes=[
                pltpu.VMEM((cap, 1), f32),
                pltpu.VMEM((cap, 1), f32),
                pltpu.VMEM((cap, width), f32),
            ],
            compiler_params=big,
            name="rows",
        )

    hidden_own, pre_own, y_own, column_own, *back_own = rows_call(f32)(
        me, u_own, g_own, router_weight, weight_in, weight_out
    )
    hidden_other, pre_other, y_other, column_other, *back_other = rows_call(bf16)(
        me, u_other, g_other, router_weight, weight_in, weight_out
    )
    back_other = [swap_dp(piece) for piece in back_other]

    def tiled(rows):
        return pl.BlockSpec((rows, tile), lambda i: (0, i))

    full = pl.BlockSpec((cap, width), lambda i: (0, 0))
    grad_weight_in, grad_weight_out = pl.pallas_call(
        weights_kernel,
        grid=(units // tile,),
        in_specs=[full, full, tiled(cap), tiled(cap), tiled(cap), tiled(cap), full, full],
        out_specs=[
            pl.BlockSpec((1, width, tile), lambda i: (0, 0, i)),
            pl.BlockSpec((1, tile, width), lambda i: (0, i, 0)),
        ],
        out_shape=[shape(weight_in.shape, bf16), shape(weight_out.shape, bf16)],
        scratch_shapes=[pltpu.VMEM((width, 2 * cap), bf16)],
        compiler_params=big,
        name="weights",
    )(u_own, u_other, pre_own, pre_other, hidden_own, hidden_other, y_own, y_other)

    column = column_own + column_other
    columns = lax.all_to_all(
        jnp.broadcast_to(column, (halves * experts, width)), ("dp", "expert"), 0, 0, tiled=True
    )
    grad_router = jnp.sum(columns.reshape(halves, experts, width), axis=0).T

    spread_rows = pl.pallas_call(
        spread_kernel,
        out_shape=[shape((most, part), bf16)] * experts,
        compiler_params=big,
        name="spread",
    )
    returned = []
    for own, other in zip(back_own, back_other):
        returned += exchange(spread_rows(compact, own, other))
    grad_tokens, grad_mod = pl.pallas_call(
        final_kernel,
        out_shape=[shape((tok_count, width), bf16), shape((1, 2, width), f32)],
        compiler_params=big,
        name="final",
    )(select, tokens, modulation[0], grad_out, *returned)
    return (grad_tokens, grad_mod, grad_router, grad_weight_in, grad_weight_out)


def solution(mesh):
    placed = (
        P(("dp", "expert"), None),
        P(("dp", "expert"), None, None),
        P(),
        P("expert", None, "dp"),
        P("expert", "dp", None),
        P("dp", None, None),
        P(("dp", "expert"), None),
    )
    return jax.shard_map(
        body,
        mesh=mesh,
        in_specs=placed,
        out_specs=(
            P(("dp", "expert"), None),
            P(("dp", "expert"), None, None),
            P(),
            P("expert", None, "dp"),
            P("expert", "dp", None),
        ),
        check_vma=False,
    )
```

```python
import jax
import jax.numpy as jnp
from jax import lax
from jax.experimental import pallas as pl
from jax.experimental.pallas import tpu as pltpu
from jax.sharding import PartitionSpec as P

gelu_root = 0.7978845608028654
gelu_cube = 0.044715
norm_eps = 1e-06
bf16, f32, i32 = jnp.bfloat16, jnp.float32, jnp.int32


def gelu_both(values):
    tangent = jnp.tanh(gelu_root * (values + gelu_cube * values * values * values))
    value = 0.5 * values * (1.0 + tangent)
    slope = 0.5 * (1.0 + tangent) + 0.5 * values * (1.0 - tangent * tangent) * gelu_root * (
        1.0 + 3.0 * gelu_cube * values * values
    )
    return value, slope


def contract(left, right, left_dim, right_dim):
    return lax.dot_general(
        left, right, (((left_dim,), (right_dim,)), ((), ())), preferred_element_type=f32
    )


def iota(shape, dim):
    return lax.broadcasted_iota(i32, shape, dim)


def normalise(tokens):
    x_float = tokens.astype(f32)
    centred = x_float - jnp.mean(x_float, axis=1, keepdims=True)
    spread = jnp.mean(centred * centred, axis=1, keepdims=True)
    inverse = lax.rsqrt(spread + norm_eps)
    return centred * inverse, inverse


def prep_kernel(me_ref, chosen_ref, tokens_ref, mod_ref, grad_ref, *outs):
    experts, cap = chosen_ref.shape
    tok_count = tokens_ref.shape[0]
    most = 2 * tok_count // experts
    shift = tok_count.bit_length() - 1
    u_outs = outs[:experts]
    g_out, select_ref, compact_u_ref, compact_g_ref, spread_ref, slot_ref = outs[experts:]
    me = me_ref[0]

    lanes = max(128, experts)
    padded = chosen_ref[...]
    if lanes > experts:
        padded = jnp.concatenate([padded, jnp.zeros((lanes - experts, cap), i32)], axis=0)
    listed = jnp.transpose(padded)
    local = listed - me * tok_count
    token_row = iota((cap, tok_count), 1)
    member = [
        jnp.sum((local[:, e : e + 1] == token_row).astype(f32), axis=0, keepdims=True)
        for e in range(experts)
    ]
    member = jnp.concatenate(member, axis=0)
    before = (iota((tok_count, tok_count), 0) < iota((tok_count, tok_count), 1)).astype(bf16)
    rank = contract(member.astype(bf16), before, 1, 0)
    slot = jnp.where(member > 0.5, rank.astype(i32), -1)
    slot_ref[...] = slot
    slot_id = iota((most, tok_count), 0)

    def one_hot(row):
        return (row == slot_id).astype(f32).astype(bf16)

    normed, _ = normalise(tokens_ref[...])
    mod = mod_ref[...].astype(f32)
    normal_u = (normed * (1.0 + mod[1:2]) + mod[0:1]).astype(bf16)
    crossed = jnp.concatenate(
        [one_hot(slot_ref[pl.ds(me ^ k, 1), :]) for k in range(experts)], axis=0
    )
    sent = contract(crossed, normal_u, 1, 0).astype(bf16)
    for k in range(experts):
        u_outs[k][...] = sent[k * most : (k + 1) * most]
    select = jnp.concatenate([one_hot(slot[e : e + 1]) for e in range(experts)], axis=0)
    select_ref[...] = select
    g_out[...] = contract(select, grad_ref[...], 1, 0).astype(bf16)

    mine = jnp.sum(jnp.where(iota((cap, lanes), 1) == me, listed, 0), axis=1, keepdims=True)
    image = lax.shift_right_logical(mine, shift)
    lane = iota((1, experts * most), 1)
    block = lax.shift_right_logical(lane, most.bit_length() - 1)
    offset = lane & (most - 1)

    def places(source):
        count = jnp.sum((image == source).astype(f32), axis=0, keepdims=True).astype(i32)
        start = jnp.sum((image < source).astype(f32), axis=0, keepdims=True).astype(i32)
        place = jnp.where(offset < count, start + offset, -1)
        return (iota((cap, experts * most), 0) == place).astype(f32)

    compact_u_ref[...] = places(block ^ me).astype(bf16)
    ordered = places(block)
    compact_g_ref[...] = ordered.astype(bf16)
    spread_ref[...] = jnp.transpose(ordered).astype(bf16)


scalar_spec = pl.BlockSpec(memory_space=pltpu.SMEM)
big = pltpu.CompilerParams(vmem_limit_bytes=56 * 1024 * 1024)


def swap_dp(values):
    count = lax.axis_size("dp")
    return lax.ppermute(values, "dp", [(i, count - 1 - i) for i in range(count)])


def pairwise(blocks):
    count = len(blocks)
    got = {0: blocks[0]}
    for k in range(count - 1, 0, -1):
        got[k] = lax.ppermute(blocks[k], "expert", [(i, i ^ k) for i in range(count)])
    return jnp.concatenate([got[k] for k in range(count)], axis=0)


def exchange(rows, experts):
    blocks = rows.reshape(experts, -1, rows.shape[1])
    return lax.all_to_all(blocks, "expert", 0, 0, tiled=True).reshape(rows.shape)


def expert_rows(rows_u, rows_g, router_weight, router_col, me, first_w, second_w):
    probs = jax.nn.sigmoid(contract(rows_u, router_weight, 1, 0)).astype(bf16).astype(f32)
    gate = jnp.sum(jnp.where(iota(probs.shape, 1) == me, probs, 0.0), axis=1, keepdims=True)
    preact = contract(rows_u, first_w, 1, 0)
    value, slope = gelu_both(preact)
    hidden = value.astype(bf16)
    upstream = contract(rows_g, second_w, 1, 1)
    score_part = jnp.sum(hidden.astype(f32) * upstream, axis=1, keepdims=True)
    grad_y = (gate * rows_g.astype(f32)).astype(bf16)
    grad_pre = (gate * upstream * slope).astype(bf16)
    logit_part = score_part * gate * (1.0 - gate)
    rows_part = contract(grad_pre, first_w, 1, 1) + logit_part * router_col
    column = jnp.sum(rows_u.astype(f32) * logit_part, axis=0)
    return hidden, grad_y, grad_pre, rows_part, column


def body(tokens, modulation, router_weight, weight_in, weight_out, chosen, grad_out):
    tok_count, width = tokens.shape
    experts = lax.axis_size("expert")
    halves = lax.axis_size("dp")
    most = 2 * tok_count // experts
    cap = chosen.shape[2]
    me = lax.axis_index("expert").astype(i32)
    shape = jax.ShapeDtypeStruct
    slots = experts * most

    *u_blocks, g_sent, select, compact_u, compact_g, spread = pl.pallas_call(
        prep_kernel,
        in_specs=[scalar_spec] + [pl.BlockSpec()] * 4,
        out_shape=[shape((most, width), bf16)] * experts
        + [
            shape((slots, width), bf16),
            shape((slots, tok_count), bf16),
            shape((cap, slots), bf16),
            shape((cap, slots), bf16),
            shape((slots, cap), bf16),
        ],
        scratch_shapes=[pltpu.VMEM((experts, tok_count), i32)],
        compiler_params=big,
        name="prep",
    )(me.reshape(1), chosen[0], tokens, modulation[0], grad_out)

    u_own = contract(compact_u, pairwise(u_blocks), 1, 0).astype(bf16)
    u_other = swap_dp(u_own)
    g_own = contract(compact_g, exchange(g_sent, experts), 1, 0).astype(bf16)
    g_other = swap_dp(g_own)

    first_w, second_w = weight_in[0], weight_out[0]
    router_col = lax.dynamic_index_in_dim(router_weight, me, 1, keepdims=False).astype(f32)
    shared = (router_weight, router_col, me, first_w, second_w)
    hidden_own, y_own, pre_own, back_own, column_own = expert_rows(u_own, g_own, *shared)
    hidden_other, y_other, pre_other, back_other, column_other = expert_rows(
        u_other, g_other, *shared
    )

    total = (back_own + swap_dp(back_other.astype(bf16)).astype(f32)).astype(bf16)
    returned = exchange(contract(spread, total, 1, 0).astype(bf16), experts)

    columns = lax.all_to_all(
        jnp.broadcast_to(column_own + column_other, (halves * experts, width)),
        ("dp", "expert"), 0, 0, tiled=True,
    )
    grad_router = jnp.sum(columns.reshape(halves, experts, width), axis=0).T

    rows_u = jnp.concatenate([u_own, u_other], axis=0)
    hidden = jnp.concatenate([hidden_own, hidden_other], axis=0)
    grad_pre = jnp.concatenate([pre_own, pre_other], axis=0)
    grad_y = jnp.concatenate([y_own, y_other], axis=0)
    grad_weight_in = contract(rows_u, grad_pre, 0, 0).astype(bf16)[None]
    grad_weight_out = contract(hidden, grad_y, 0, 0).astype(bf16)[None]

    grad_u = contract(select, returned, 0, 0)
    normed, inverse = normalise(tokens)
    scale_mod = modulation[0, 1].astype(f32)
    grad_shift = jnp.sum(grad_u, axis=0)
    grad_scale = jnp.sum(grad_u * normed, axis=0)
    grad_mod = jnp.stack([grad_shift, grad_scale], axis=0)[None]
    grad_norm = grad_u * (1.0 + scale_mod)
    centre_term = jnp.mean(grad_norm, axis=1, keepdims=True)
    slope_term = jnp.mean(grad_norm * normed, axis=1, keepdims=True)
    grad_tokens = (
        grad_out.astype(f32) + (grad_norm - centre_term - normed * slope_term) * inverse
    ).astype(bf16)
    return (grad_tokens, grad_mod, grad_router, grad_weight_in, grad_weight_out)


def solution(mesh):
    placed = (
        P(("dp", "expert"), None),
        P(("dp", "expert"), None, None),
        P(),
        P("expert", None, "dp"),
        P("expert", "dp", None),
        P("dp", None, None),
        P(("dp", "expert"), None),
    )
    return jax.shard_map(
        body,
        mesh=mesh,
        in_specs=placed,
        out_specs=(
            P(("dp", "expert"), None),
            P(("dp", "expert"), None, None),
            P(),
            P("expert", None, "dp"),
            P("expert", "dp", None),
        ),
        check_vma=False,
    )
```

```python
import functools

import jax
import jax.numpy as jnp
from jax import lax
from jax.experimental import pallas as pl
from jax.experimental.pallas import tpu as pltpu
from jax.sharding import PartitionSpec as P

gelu_root = 0.7978845608028654
gelu_cube = 0.044715
norm_eps = 1e-06
bf16, f32, i32 = jnp.bfloat16, jnp.float32, jnp.int32


def gelu_both(values):
    tangent = jnp.tanh(gelu_root * (values + gelu_cube * values * values * values))
    value = 0.5 * values * (1.0 + tangent)
    slope = 0.5 * (1.0 + tangent) + 0.5 * values * (1.0 - tangent * tangent) * gelu_root * (
        1.0 + 3.0 * gelu_cube * values * values
    )
    return value, slope


def contract(left, right, left_dim, right_dim):
    return lax.dot_general(
        left, right, (((left_dim,), (right_dim,)), ((), ())), preferred_element_type=f32
    )


def iota(shape, dim):
    return lax.broadcasted_iota(i32, shape, dim)


def normalise(tokens):
    x_float = tokens.astype(f32)
    centred = x_float - jnp.mean(x_float, axis=1, keepdims=True)
    spread = jnp.mean(centred * centred, axis=1, keepdims=True)
    inverse = lax.rsqrt(spread + norm_eps)
    return centred * inverse, inverse


def prep_u_kernel(me_ref, chosen_ref, tokens_ref, mod_ref, *outs):
    experts, cap = chosen_ref.shape
    tok_count = tokens_ref.shape[0]
    most = 2 * tok_count // experts
    *u_outs, select_ref, slot_ref = outs
    me = me_ref[0]

    lanes = max(128, experts)
    padded = chosen_ref[...]
    if lanes > experts:
        padded = jnp.concatenate([padded, jnp.zeros((lanes - experts, cap), i32)], axis=0)
    local = jnp.transpose(padded) - me * tok_count
    token_row = iota((cap, tok_count), 1)
    member = [
        jnp.sum((local[:, e : e + 1] == token_row).astype(f32), axis=0, keepdims=True)
        for e in range(experts)
    ]
    member = jnp.concatenate(member, axis=0)
    before = (iota((tok_count, tok_count), 0) < iota((tok_count, tok_count), 1)).astype(bf16)
    rank = contract(member.astype(bf16), before, 1, 0)
    slot = jnp.where(member > 0.5, rank.astype(i32), -1)
    slot_ref[...] = slot
    slot_id = iota((most, tok_count), 0)

    def one_hot(row):
        return (row == slot_id).astype(f32).astype(bf16)

    normed, _ = normalise(tokens_ref[...])
    mod = mod_ref[...].astype(f32)
    normal_u = (normed * (1.0 + mod[1:2]) + mod[0:1]).astype(bf16)
    crossed = jnp.concatenate(
        [one_hot(slot_ref[pl.ds(me ^ k, 1), :]) for k in range(experts)], axis=0
    )
    sent = contract(crossed, normal_u, 1, 0).astype(bf16)
    for k in range(experts):
        u_outs[k][...] = sent[k * most : (k + 1) * most]
    for e in range(experts):
        select_ref[e * most : (e + 1) * most, :] = one_hot(slot[e : e + 1])


def prep_g_kernel(most, me_ref, chosen_ref, select_ref, grad_ref, g_out, u_place, g_place, spread):
    _, cap = chosen_ref.shape
    slots, tok_count = select_ref.shape
    me = me_ref[0]
    g_out[...] = contract(select_ref[...], grad_ref[...], 1, 0).astype(bf16)

    row = chosen_ref[pl.ds(me, 1), :]
    mine = jnp.transpose(jnp.concatenate([row] * 128, axis=0))[:, 0:1]
    image = lax.shift_right_logical(mine, tok_count.bit_length() - 1)
    lane = iota((1, slots), 1)
    block = lax.shift_right_logical(lane, most.bit_length() - 1)
    offset = lane & (most - 1)

    def places(source):
        count = jnp.sum((image == source).astype(f32), axis=0, keepdims=True).astype(i32)
        start = jnp.sum((image < source).astype(f32), axis=0, keepdims=True).astype(i32)
        place = jnp.where(offset < count, start + offset, -1)
        return (iota((cap, slots), 0) == place).astype(f32)

    u_place[...] = places(block ^ me).astype(bf16)
    ordered = places(block)
    g_place[...] = ordered.astype(bf16)
    spread[...] = jnp.transpose(ordered).astype(bf16)


scalar_spec = pl.BlockSpec(memory_space=pltpu.SMEM)
big = pltpu.CompilerParams(vmem_limit_bytes=56 * 1024 * 1024)


def swap_dp(values):
    count = lax.axis_size("dp")
    return lax.ppermute(values, "dp", [(i, count - 1 - i) for i in range(count)])


def pairwise(blocks):
    count = len(blocks)
    got = {0: blocks[0]}
    for k in range(count - 1, 0, -1):
        got[k] = lax.ppermute(blocks[k], "expert", [(i, i ^ k) for i in range(count)])
    return jnp.concatenate([got[k] for k in range(count)], axis=0)


def exchange(rows, experts):
    blocks = rows.reshape(experts, -1, rows.shape[1])
    return lax.all_to_all(blocks, "expert", 0, 0, tiled=True).reshape(rows.shape)


def expert_rows(rows_u, rows_g, router_weight, router_col, me, first_w, second_w):
    probs = jax.nn.sigmoid(contract(rows_u, router_weight, 1, 0)).astype(bf16).astype(f32)
    gate = jnp.sum(jnp.where(iota(probs.shape, 1) == me, probs, 0.0), axis=1, keepdims=True)
    preact = contract(rows_u, first_w, 1, 0)
    value, slope = gelu_both(preact)
    hidden = value.astype(bf16)
    upstream = contract(rows_g, second_w, 1, 1)
    score_part = jnp.sum(hidden.astype(f32) * upstream, axis=1, keepdims=True)
    grad_y = (gate * rows_g.astype(f32)).astype(bf16)
    grad_pre = (gate * upstream * slope).astype(bf16)
    logit_part = score_part * gate * (1.0 - gate)
    rows_part = contract(grad_pre, first_w, 1, 1) + logit_part * router_col
    column = jnp.sum(rows_u.astype(f32) * logit_part, axis=0)
    return hidden, grad_y, grad_pre, rows_part, column


def body(tokens, modulation, router_weight, weight_in, weight_out, chosen, grad_out):
    tok_count, width = tokens.shape
    experts = lax.axis_size("expert")
    halves = lax.axis_size("dp")
    most = 2 * tok_count // experts
    cap = chosen.shape[2]
    me = lax.axis_index("expert").astype(i32)
    shape = jax.ShapeDtypeStruct
    slots = experts * most

    *u_blocks, select = pl.pallas_call(
        prep_u_kernel,
        in_specs=[scalar_spec] + [pl.BlockSpec()] * 3,
        out_shape=[shape((most, width), bf16)] * experts + [shape((slots, tok_count), bf16)],
        scratch_shapes=[pltpu.VMEM((experts, tok_count), i32)],
        compiler_params=big,
        name="prep_u",
    )(me.reshape(1), chosen[0], tokens, modulation[0])
    g_sent, u_place, g_place, spread = pl.pallas_call(
        functools.partial(prep_g_kernel, most),
        in_specs=[scalar_spec] + [pl.BlockSpec()] * 3,
        out_shape=[
            shape((slots, width), bf16),
            shape((cap, slots), bf16),
            shape((cap, slots), bf16),
            shape((slots, cap), bf16),
        ],
        compiler_params=big,
        name="prep_g",
    )(me.reshape(1), chosen[0], select, grad_out)

    g_got = exchange(g_sent, experts)
    u_own = contract(u_place, pairwise(u_blocks), 1, 0).astype(bf16)
    u_other = swap_dp(u_own)
    g_own = contract(g_place, g_got, 1, 0).astype(bf16)
    g_other = swap_dp(g_own)

    first_w, second_w = weight_in[0], weight_out[0]
    router_col = lax.dynamic_index_in_dim(router_weight, me, 1, keepdims=False).astype(f32)
    shared = (router_weight, router_col, me, first_w, second_w)
    hidden_own, y_own, pre_own, back_own, column_own = expert_rows(u_own, g_own, *shared)
    back_own, column_own, g_other = lax.optimization_barrier((back_own, column_own, g_other))
    hidden_other, y_other, pre_other, back_other, column_other = expert_rows(
        u_other, g_other, *shared
    )

    total = (back_own + swap_dp(back_other.astype(bf16)).astype(f32)).astype(bf16)
    returned = exchange(contract(spread, total, 1, 0).astype(bf16), experts)

    columns = lax.all_to_all(
        jnp.broadcast_to(column_own + column_other, (halves * experts, width)),
        ("dp", "expert"), 0, 0, tiled=True,
    )
    grad_router = jnp.sum(columns.reshape(halves, experts, width), axis=0).T

    rows_u = jnp.concatenate([u_own, u_other], axis=0)
    hidden = jnp.concatenate([hidden_own, hidden_other], axis=0)
    grad_pre = jnp.concatenate([pre_own, pre_other], axis=0)
    grad_y = jnp.concatenate([y_own, y_other], axis=0)
    grad_weight_in = contract(rows_u, grad_pre, 0, 0).astype(bf16)[None]
    grad_weight_out = contract(hidden, grad_y, 0, 0).astype(bf16)[None]

    grad_u = contract(select, returned, 0, 0)
    normed, inverse = normalise(tokens)
    scale_mod = modulation[0, 1].astype(f32)
    grad_shift = jnp.sum(grad_u, axis=0)
    grad_scale = jnp.sum(grad_u * normed, axis=0)
    grad_mod = jnp.stack([grad_shift, grad_scale], axis=0)[None]
    grad_norm = grad_u * (1.0 + scale_mod)
    centre_term = jnp.mean(grad_norm, axis=1, keepdims=True)
    slope_term = jnp.mean(grad_norm * normed, axis=1, keepdims=True)
    grad_tokens = (
        grad_out.astype(f32) + (grad_norm - centre_term - normed * slope_term) * inverse
    ).astype(bf16)
    return (grad_tokens, grad_mod, grad_router, grad_weight_in, grad_weight_out)


def solution(mesh):
    placed = (
        P(("dp", "expert"), None),
        P(("dp", "expert"), None, None),
        P(),
        P("expert", None, "dp"),
        P("expert", "dp", None),
        P("dp", None, None),
        P(("dp", "expert"), None),
    )
    return jax.shard_map(
        body,
        mesh=mesh,
        in_specs=placed,
        out_specs=(
            P(("dp", "expert"), None),
            P(("dp", "expert"), None, None),
            P(),
            P("expert", None, "dp"),
            P("expert", "dp", None),
        ),
        check_vma=False,
    )
```

```python
import functools

import jax
import jax.numpy as jnp
from jax import lax
from jax.experimental import pallas as pl
from jax.experimental.pallas import tpu as pltpu
from jax.sharding import PartitionSpec as P

gelu_root = 0.7978845608028654
gelu_cube = 0.044715
norm_eps = 1e-06
bf16, f32, i32 = jnp.bfloat16, jnp.float32, jnp.int32


def gelu_both(values):
    tangent = jnp.tanh(gelu_root * (values + gelu_cube * values * values * values))
    value = 0.5 * values * (1.0 + tangent)
    slope = 0.5 * (1.0 + tangent) + 0.5 * values * (1.0 - tangent * tangent) * gelu_root * (
        1.0 + 3.0 * gelu_cube * values * values
    )
    return value, slope


def contract(left, right, left_dim, right_dim):
    return lax.dot_general(
        left, right, (((left_dim,), (right_dim,)), ((), ())), preferred_element_type=f32
    )


def iota(shape, dim):
    return lax.broadcasted_iota(i32, shape, dim)


def normalise(tokens):
    x_float = tokens.astype(f32)
    centred = x_float - jnp.mean(x_float, axis=1, keepdims=True)
    spread = jnp.mean(centred * centred, axis=1, keepdims=True)
    inverse = lax.rsqrt(spread + norm_eps)
    return centred * inverse, inverse


def prep_u_kernel(me_ref, chosen_ref, tokens_ref, mod_ref, *outs):
    experts, cap = chosen_ref.shape
    tok_count = tokens_ref.shape[0]
    most = 2 * tok_count // experts
    *u_outs, select_ref, slot_ref = outs
    me = me_ref[0]

    lanes = max(128, experts)
    padded = chosen_ref[...]
    if lanes > experts:
        padded = jnp.concatenate([padded, jnp.zeros((lanes - experts, cap), i32)], axis=0)
    local = jnp.transpose(padded) - me * tok_count
    token_row = iota((cap, tok_count), 1)
    member = [
        jnp.sum((local[:, e : e + 1] == token_row).astype(f32), axis=0, keepdims=True)
        for e in range(experts)
    ]
    member = jnp.concatenate(member, axis=0)
    before = (iota((tok_count, tok_count), 0) < iota((tok_count, tok_count), 1)).astype(bf16)
    rank = contract(member.astype(bf16), before, 1, 0)
    slot = jnp.where(member > 0.5, rank.astype(i32), -1)
    slot_ref[...] = slot
    slot_id = iota((most, tok_count), 0)

    def one_hot(row):
        return (row == slot_id).astype(f32).astype(bf16)

    normed, _ = normalise(tokens_ref[...])
    mod = mod_ref[...].astype(f32)
    normal_u = (normed * (1.0 + mod[1:2]) + mod[0:1]).astype(bf16)
    crossed = jnp.concatenate(
        [one_hot(slot_ref[pl.ds(me ^ k, 1), :]) for k in range(experts)], axis=0
    )
    sent = contract(crossed, normal_u, 1, 0).astype(bf16)
    for k in range(len(u_outs)):
        u_outs[k][...] = sent[2 * k * most : 2 * (k + 1) * most]
    for e in range(experts):
        select_ref[e * most : (e + 1) * most, :] = one_hot(slot[e : e + 1])


def prep_g_kernel(most, me_ref, chosen_ref, select_ref, grad_ref, g_out, u_place, g_place, spread):
    experts, cap = chosen_ref.shape
    slots, tok_count = select_ref.shape
    me = me_ref[0]
    g_out[...] = contract(select_ref[...], grad_ref[...], 1, 0).astype(bf16)

    row = chosen_ref[pl.ds(me, 1), :]
    mine = jnp.transpose(jnp.concatenate([row] * 128, axis=0))[:, 0:1]
    image = lax.shift_right_logical(mine, tok_count.bit_length() - 1)
    lane = iota((1, slots), 1)
    block = lax.shift_right_logical(lane, most.bit_length() - 1)
    offset = lane & (most - 1)

    def places(source):
        count = jnp.sum((image == source).astype(f32), axis=0, keepdims=True).astype(i32)
        start = jnp.sum((image < source).astype(f32), axis=0, keepdims=True).astype(i32)
        place = jnp.where(offset < count, start + offset, -1)
        return (iota((cap, slots), 0) == place).astype(f32)

    half = experts // 2
    turn = jnp.where(block < half, 2 * block, 2 * (block - half) + 1)
    u_place[...] = places(turn ^ me).astype(bf16)
    ordered = places(block)
    g_place[...] = ordered.astype(bf16)
    spread[...] = jnp.transpose(ordered).astype(bf16)


scalar_spec = pl.BlockSpec(memory_space=pltpu.SMEM)
big = pltpu.CompilerParams(vmem_limit_bytes=56 * 1024 * 1024)


def swap_dp(values):
    count = lax.axis_size("dp")
    return lax.ppermute(values, "dp", [(i, count - 1 - i) for i in range(count)])


def pairwise(pairs):
    count = lax.axis_size("expert")
    most = pairs[0].shape[0] // 2
    got = {0: pairs[0]}
    for k in range(len(pairs) - 1, 0, -1):
        got[k] = lax.ppermute(pairs[k], "expert", [(i, i ^ (2 * k)) for i in range(count)])
    got = [got[k] for k in range(len(pairs))]
    passed = jnp.concatenate([pair[most:] for pair in got], axis=0)
    passed = lax.ppermute(passed, "expert", [(i, i ^ 1) for i in range(count)])
    return jnp.concatenate([pair[:most] for pair in got] + [passed], axis=0)


def exchange(rows, experts):
    blocks = rows.reshape(experts, -1, rows.shape[1])
    return lax.all_to_all(blocks, "expert", 0, 0, tiled=True).reshape(rows.shape)


def expert_rows(rows_u, rows_g, router_weight, router_col, me, first_w, second_w):
    probs = jax.nn.sigmoid(contract(rows_u, router_weight, 1, 0)).astype(bf16).astype(f32)
    gate = jnp.sum(jnp.where(iota(probs.shape, 1) == me, probs, 0.0), axis=1, keepdims=True)
    preact = contract(rows_u, first_w, 1, 0)
    value, slope = gelu_both(preact)
    hidden = value.astype(bf16)
    upstream = contract(rows_g, second_w, 1, 1)
    score_part = jnp.sum(hidden.astype(f32) * upstream, axis=1, keepdims=True)
    grad_y = (gate * rows_g.astype(f32)).astype(bf16)
    grad_pre = (gate * upstream * slope).astype(bf16)
    logit_part = score_part * gate * (1.0 - gate)
    rows_part = contract(grad_pre, first_w, 1, 1) + logit_part * router_col
    column = jnp.sum(rows_u.astype(f32) * logit_part, axis=0)
    return hidden, grad_y, grad_pre, rows_part, column


def body(tokens, modulation, router_weight, weight_in, weight_out, chosen, grad_out):
    tok_count, width = tokens.shape
    experts = lax.axis_size("expert")
    most = 2 * tok_count // experts
    cap = chosen.shape[2]
    me = lax.axis_index("expert").astype(i32)
    shape = jax.ShapeDtypeStruct
    slots = experts * most

    *u_blocks, select = pl.pallas_call(
        prep_u_kernel,
        in_specs=[scalar_spec] + [pl.BlockSpec()] * 3,
        out_shape=[shape((2 * most, width), bf16)] * (experts // 2)
        + [shape((slots, tok_count), bf16)],
        scratch_shapes=[pltpu.VMEM((experts, tok_count), i32)],
        compiler_params=big,
        name="prep_u",
    )(me.reshape(1), chosen[0], tokens, modulation[0])
    g_sent, u_place, g_place, spread = pl.pallas_call(
        functools.partial(prep_g_kernel, most),
        in_specs=[scalar_spec] + [pl.BlockSpec()] * 3,
        out_shape=[
            shape((slots, width), bf16),
            shape((cap, slots), bf16),
            shape((cap, slots), bf16),
            shape((slots, cap), bf16),
        ],
        compiler_params=big,
        name="prep_g",
    )(me.reshape(1), chosen[0], select, grad_out)

    g_got = exchange(g_sent, experts)
    u_own = contract(u_place, pairwise(u_blocks), 1, 0).astype(bf16)
    u_other = swap_dp(u_own)
    g_own = contract(g_place, g_got, 1, 0).astype(bf16)
    g_other = swap_dp(g_own)

    first_w, second_w = weight_in[0], weight_out[0]
    router_col = lax.dynamic_index_in_dim(router_weight, me, 1, keepdims=False).astype(f32)
    shared = (router_weight, router_col, me, first_w, second_w)
    hidden_own, y_own, pre_own, back_own, column_own = expert_rows(u_own, g_own, *shared)
    back_own, column_own, g_other = lax.optimization_barrier((back_own, column_own, g_other))
    hidden_other, y_other, pre_other, back_other, column_other = expert_rows(
        u_other, g_other, *shared
    )

    total = (back_own + swap_dp(back_other.astype(bf16)).astype(f32)).astype(bf16)
    total = lax.optimization_barrier(total)
    returned = exchange(contract(spread, total, 1, 0).astype(bf16), experts)

    columns = lax.all_to_all(
        jnp.broadcast_to(column_own + column_other, (experts, width)), "expert", 0, 0, tiled=True
    )
    grad_router = (columns + swap_dp(columns)).T

    rows_u = jnp.concatenate([u_own, u_other], axis=0)
    hidden = jnp.concatenate([hidden_own, hidden_other], axis=0)
    grad_pre = jnp.concatenate([pre_own, pre_other], axis=0)
    grad_y = jnp.concatenate([y_own, y_other], axis=0)
    grad_weight_in = contract(rows_u, grad_pre, 0, 0).astype(bf16)[None]
    grad_weight_out = contract(hidden, grad_y, 0, 0).astype(bf16)[None]

    grad_u = contract(select, returned, 0, 0)
    normed, inverse = normalise(tokens)
    scale_mod = modulation[0, 1].astype(f32)
    grad_shift = jnp.sum(grad_u, axis=0)
    grad_scale = jnp.sum(grad_u * normed, axis=0)
    grad_mod = jnp.stack([grad_shift, grad_scale], axis=0)[None]
    grad_norm = grad_u * (1.0 + scale_mod)
    centre_term = jnp.mean(grad_norm, axis=1, keepdims=True)
    slope_term = jnp.mean(grad_norm * normed, axis=1, keepdims=True)
    grad_tokens = (
        grad_out.astype(f32) + (grad_norm - centre_term - normed * slope_term) * inverse
    ).astype(bf16)
    return (grad_tokens, grad_mod, grad_router, grad_weight_in, grad_weight_out)


def solution(mesh):
    placed = (
        P(("dp", "expert"), None),
        P(("dp", "expert"), None, None),
        P(),
        P("expert", None, "dp"),
        P("expert", "dp", None),
        P("dp", None, None),
        P(("dp", "expert"), None),
    )
    return jax.shard_map(
        body,
        mesh=mesh,
        in_specs=placed,
        out_specs=(
            P(("dp", "expert"), None),
            P(("dp", "expert"), None, None),
            P(),
            P("expert", None, "dp"),
            P("expert", "dp", None),
        ),
        check_vma=False,
    )
```
